768 devices in a mesh: dp: 96 (over y, z_hi, x), tensor: 8 (over z_lo, core).
Axes of the slice: x: 4, y: 8, z: 12 (z_hi: 3, z_lo: 4; z = z_hi * 4 + z_lo), core: 2. Of those that a mesh axis runs over, the one named last changes fastest.
Arguments:
- d_out: bfloat16 [96, 1024, 2560], P('dp', 'tensor'), may hold values from -12 to 12
- attn_out: bfloat16 [96, 1024, 3072], P('dp', None, 'tensor'), may hold values from -20 to 20
- queries: bfloat16 [96, 1024, 3072], P('dp', None, 'tensor'), may hold values from -40 to 40
- keys: bfloat16 [96, 1024, 3072], P('dp', None, 'tensor'), may hold values from -4 to 4
- out_weight: bfloat16 [3072, 2560], P('tensor'), may hold values from -0.125 to 0.125
- segment_ids: int32 [96, 1024], P('dp'), may hold values from 0 to 2, as said below
Outputs:
- value_grad: bfloat16 [96, 1024, 3072], P('dp', None, 'tensor')
- weight_grad: float32 [3072, 2560], P(('tensor', 'dp'))
The draws below stay inside these ranges and needn't reach their ends.
Inputs may be any that keep to these rules, and one draw needn't show every extreme that they name: `segment_ids`: ids start at 0, never fall along a sequence, and rise by one where a new document begins; exactly one new document begins in every aligned block of min(512, 1024) positions.
All inputs are finite; a program needn't handle non-finite values.
Results may differ from the reference program's by a relative error of at most 0.008.
Values may be sent and summed in bfloat16 or wider, within the bound.
No kernel may reach another device: no remote copies, remote signals or barrier semaphores. Data moves between devices by JAX's collectives and lax.ppermute only.
A program may use at most 64 MiB of HBM per device.

```python
import jax
import jax.numpy as jnp
from jax import lax

D = 2560
HEADS = 24
HEAD_DIM = 128
L = 1024
SEQS = 96
ATTN_WIDTH = 3072


def common_draw(key):
    block_len = min(512, L)
    block_count = L // block_len
    offset_any = jax.random.randint(jax.random.fold_in(key, 101), (SEQS, block_count), 0, block_len)
    offset_first = jax.random.randint(jax.random.fold_in(key, 111), (SEQS, block_count), 1, block_len)
    block_index = jnp.arange(block_count)[None, :]
    offsets = jnp.where(block_index == 0, offset_first, offset_any)
    inside = jnp.arange(block_len)[None, None, :]
    starts = (inside == offsets[:, :, None]).reshape(SEQS, L)
    segments = jnp.cumsum(starts.astype(jnp.int32), axis=1).astype(jnp.int32)
    seed_query = jax.random.fold_in(key, 202)
    seed_keys = jax.random.fold_in(key, 303)
    shape_heads = (SEQS, L, HEADS, HEAD_DIM)
    query_full = jnp.clip(jax.random.normal(seed_query, shape_heads, jnp.float32), -4.0, 4.0)
    key_full = jnp.clip(jax.random.normal(seed_keys, shape_heads, jnp.float32), -4.0, 4.0)
    width_all = HEADS * HEAD_DIM
    return (segments, query_full.reshape(SEQS, L, width_all), key_full.reshape(SEQS, L, width_all))


def draw_segment_ids(key, part):
    return common_draw(key)[0]


def draw_queries(key, part):
    return common_draw(key)[1].astype(jnp.bfloat16)


def draw_keys(key, part):
    return common_draw(key)[2].astype(jnp.bfloat16)


def spiked(drawn, key, source, target, parts, factor):
    def block_of(axis_at):
        return (jnp.arange(drawn.shape[axis_at]) // (drawn.shape[axis_at] // parts)).reshape((-1,) + (1,) * (drawn.ndim - 1 - axis_at))

    near = jax.random.permutation(key, parts)[block_of(target)]
    far = (block_of(target) + parts // 2) % parts
    return jnp.where((block_of(source) == near) | (block_of(source) == far), factor * drawn, drawn)


def shard_levels(rng, shape, pieces, least, largest):
    loudness, own = 1.0, jax.random.fold_in(rng, 6)
    for dim, parts in pieces:
        heights = jnp.exp(jax.random.uniform(jax.random.fold_in(own, dim), (parts,), jnp.float32, least / len(pieces), largest / len(pieces)))
        loudness = loudness * jnp.repeat(heights, shape[dim] // parts).reshape([-1 if axis == dim else 1 for axis in range(len(shape))])
    return loudness


def centred(own_key, extent, deviation, most, pieces=(), kind=jnp.bfloat16):
    drawn = jax.random.normal(own_key, extent, jnp.float32) * deviation
    if len(pieces) > 0:
        drawn = shard_levels(own_key, extent, pieces, -0.22, 0.18) * drawn
    return jnp.clip(drawn, min=-most, max=most).astype(kind)


def heavy_noise(key, shape, deviation, most, shards, heavy, held_as=jnp.bfloat16):
    array = deviation * jax.random.normal(key, shape, jnp.float32)
    if shards:
        array = array * shard_levels(key, shape, shards, -0.22, 0.18)
    return jnp.clip(spiked(array, jax.random.fold_in(key, 3), *heavy), -most, most).astype(held_as)


def setup_inputs(seed: int = 0) -> dict:
    key_of = jax.random.split(jax.random.key(seed), 7)
    d_out = centred(key_of[0], (SEQS, L, D), 2.0, 12.0, ((0, 96), (1, 8)))
    attn_out = heavy_noise(key_of[1], (SEQS, L, ATTN_WIDTH), 1.0, 20.0, ((0, 96), (2, 8)), (0, 2, 96, 4.75))
    queries = draw_queries(jax.random.fold_in(key_of[6], 71), 0)
    keys = draw_keys(jax.random.fold_in(key_of[6], 71), 0)
    out_weight = centred(key_of[4], (ATTN_WIDTH, D), D ** -0.5, 0.125, ((0, 8),))
    segment_ids = draw_segment_ids(jax.random.fold_in(key_of[6], 71), 0)
    return dict(d_out=d_out, attn_out=attn_out, queries=queries, keys=keys, out_weight=out_weight, segment_ids=segment_ids)


def value_path(attn_grad, query_rows, key_rows, segment_row):
    query_heads = query_rows.astype(jnp.float32).reshape(L, HEADS, HEAD_DIM)
    key_heads = key_rows.astype(jnp.float32).reshape(L, HEADS, HEAD_DIM)
    scores = jnp.einsum("qhd,khd->hqk", query_heads, key_heads) * (HEAD_DIM ** -0.5)
    position = jnp.arange(L)
    allowed = (position[:, None] >= position[None, :]) & (segment_row[:, None] == segment_row[None, :])
    masked = jnp.where(allowed[None], scores, -jnp.inf)
    highest = jnp.max(masked, axis=2, keepdims=True)
    weights = jnp.where(allowed[None], jnp.exp(masked - highest), 0.0)
    probabilities = (weights / jnp.sum(weights, axis=2, keepdims=True)).astype(jnp.bfloat16)
    grad_heads = attn_grad.astype(jnp.float32).reshape(L, HEADS, HEAD_DIM)
    result = jnp.einsum("hqk,qhd->khd", probabilities.astype(jnp.float32), grad_heads)
    return result.reshape(L, HEADS * HEAD_DIM).astype(jnp.bfloat16)


def reference(d_out, attn_out, queries, keys, out_weight, segment_ids):
    def one_sequence(bucket_sum, sequence_items):
        grad_rows, output_rows, query_rows, key_rows, segment_row = sequence_items
        attn_grad = jnp.dot(grad_rows, out_weight.T, preferred_element_type=jnp.float32).astype(jnp.bfloat16)
        value_rows = value_path(attn_grad, query_rows, key_rows, segment_row)
        bucket_sum = bucket_sum + jnp.dot(output_rows.T, grad_rows, preferred_element_type=jnp.float32)
        return bucket_sum, value_rows

    start_sum = jnp.zeros((HEADS * HEAD_DIM, D), jnp.float32)
    bucket_sum, value_grad = lax.scan(one_sequence, start_sum, (d_out, attn_out, queries, keys, segment_ids))
    return value_grad, bucket_sum / SEQS
```

```python
import jax
import jax.numpy as jnp
from jax import lax
from jax.experimental import pallas as pl
from jax.experimental.pallas import tpu as pltpu
from jax.sharding import PartitionSpec as P

HEAD_DIM = 128
NY, NZ, NX = 8, 3, 4
DP = NY * NZ * NX
CHUNKS = (1280, 1280)
FIRSTS = tuple(sum(CHUNKS[:i]) for i in range(len(CHUNKS)))
VMEM_LIMIT = 12 << 20


def dp_at(y, z, x):
    return (y * NZ + z) * NX + x


GROUPS_X = [[dp_at(y, z, x) for x in range(NX)] for y in range(NY) for z in range(NZ)]
GROUPS_YZ = [[dp_at(y, z, x) for y in range(NY) for z in range(NZ)] for x in range(NX)]

PAIRS = [(t, t ^ 2) for t in range(8)]
MIDDLE = [(2, 4), (3, 5), (4, 2), (5, 3)]
ENDS = [(2, 0), (3, 1), (4, 6), (5, 7)]
PARTNER = [(t, t ^ 1) for t in range(8)]

VMEM = pl.BlockSpec(memory_space=pltpu.VMEM)
SMEM = pl.BlockSpec(memory_space=pltpu.SMEM)


def local_call(kernel, out, scalars, *arrays, scratch=(), fetched=False, stored=False, limit=VMEM_LIMIT, column=()):
    def whole(array):
        return pl.BlockSpec(array.shape, lambda i: (0,) * len(array.shape), pipeline_mode=pl.Buffered(1))

    def fetch(i, array):
        if i not in column:
            return whole(array)
        shape, at = (array.shape[0], out.shape[1]), column[i]
        return pl.BlockSpec(shape, lambda i: (0, at), pipeline_mode=pl.Buffered(1))

    if fetched:
        arrays = [pltpu.with_memory_space_constraint(array, pltpu.HBM) for array in arrays]
    return pl.pallas_call(
        kernel,
        out_shape=pltpu.HBM(out.shape, out.dtype) if stored else out,
        grid=(1,) if fetched or stored else (),
        in_specs=[SMEM] * len(scalars) + [fetch(i, array) if fetched else VMEM for i, array in enumerate(arrays)],
        out_specs=whole(out) if stored else jax.tree.map(lambda _: VMEM, out),
        scratch_shapes=list(scratch),
        compiler_params=pltpu.CompilerParams(vmem_limit_bytes=limit),
    )(*scalars, *arrays)


def like(array, *shape):
    return jax.ShapeDtypeStruct(shape, array.dtype)


def block_order(tensor):
    core = tensor & 1
    low = tensor < 4
    far_a = jnp.where(low, 4, 2) + core
    far_b = jnp.where(low, 6, 0) + core
    near = tensor ^ 2
    return [tensor, tensor ^ 1, near, near ^ 1, far_a, far_a ^ 1, far_b, far_b ^ 1]


def split_kernel(whole_ref, *out_refs):
    for first, ref in zip(FIRSTS, out_refs):
        ref[...] = whole_ref[:, first : first + ref.shape[1]]


def split(whole):
    out = [like(whole, whole.shape[0], c) for c in CHUNKS]
    return local_call(split_kernel, out, [], whole)


def features_kernel(tensor_ref, select_ref, rows_ref, out_ref):
    block = out_ref.shape[1] // 8
    for i, at in enumerate(block_order(tensor_ref[0])):
        rows = rows_ref[pl.ds(pl.multiple_of(at * block, block), block), :]
        out_ref[:, i * block : (i + 1) * block] = lax.dot_general(
            select_ref[...], rows, (((1,), (1,)), ((), ())), preferred_element_type=jnp.float32
        ).astype(out_ref.dtype)


def ordered_features(tensor, outputs):
    length, width = outputs.shape
    rows = width // DP
    new = jnp.arange(width)
    x, y, z, r = new // (width // NX), new // (NZ * rows) % NY, new // rows % NZ, new % rows
    old = dp_at(y, z, x) * rows + r
    select = (old[:, None] == jnp.arange(width)[None, :]).astype(outputs.dtype)
    return local_call(features_kernel, like(outputs, width, length), [tensor], select, outputs)


def pick_kernel(tensor_ref, middle_ref, ends_ref, out_ref):
    tensor = tensor_ref[0]
    at_end = (tensor < 2) | (tensor >= 6)

    @pl.when(at_end)
    def _():
        out_ref[...] = ends_ref[...]

    @pl.when(jnp.logical_not(at_end))
    def _():
        out_ref[...] = middle_ref[...]


def pick(tensor, middle, ends):
    return local_call(pick_kernel, like(middle, *middle.shape), [tensor], middle, ends, stored=True)


def product_rows(features, whole, last, first):
    width = features.shape[0]
    cols = last[0].shape[1]

    def kernel(features_ref, *refs):
        out_ref = refs[-1]
        for at in range(0, cols, 256):
            here = slice(at, at + 256)
            blocks = [ref[:, here] for ref in refs[:-1]]
            out_ref[:, here] = jnp.dot(
                features_ref[...], jnp.concatenate(blocks, axis=0), preferred_element_type=jnp.float32
            ).astype(out_ref.dtype)

    out = jax.ShapeDtypeStruct((width, cols), jnp.bfloat16)
    column = {1 + i: first // cols for i in range(len(whole))}
    return local_call(kernel, out, [], features, *whole, *last, fetched=True, stored=True, column=column)


def probs_kernel(query_ref, key_ref, seg_col_ref, seg_row_ref, out_ref):
    length = query_ref.shape[0]
    heads = query_ref.shape[1] // HEAD_DIM
    step = out_ref.shape[1] // heads
    scale = HEAD_DIM**-0.5
    base = 0
    for first in range(0, length, step):
        stop = first + step
        key_at = lax.broadcasted_iota(jnp.int32, (stop, step), 0)
        query_at = lax.broadcasted_iota(jnp.int32, (stop, step), 1) + first
        allowed = (key_at <= query_at) & (seg_col_ref[0:stop, :] == seg_row_ref[:, first:stop])
        bias = jnp.where(allowed, 0.0, -1e30)
        for head in range(heads):
            cols = slice(head * HEAD_DIM, (head + 1) * HEAD_DIM)
            scores = lax.dot_general(
                key_ref[0:stop, cols],
                query_ref[first:stop, cols],
                (((1,), (1,)), ((), ())),
                preferred_element_type=jnp.float32,
            )
            masked = scores + bias
            highest = jnp.max(masked, axis=0, keepdims=True)
            weights = jnp.exp((masked - highest) * scale)
            inverse = 1.0 / jnp.sum(weights, axis=0, keepdims=True)
            out_ref[base : base + stop, head * step : (head + 1) * step] = (weights * inverse).astype(out_ref.dtype)
        base += stop


def probs_columns(queries, keys, segments):
    length, width = queries.shape
    step = min(256, length)
    spans = sum(range(step, length + 1, step))
    out = like(queries, spans, width // HEAD_DIM * step)
    arrays = (queries, keys, segments[:, None], segments[None, :])
    return local_call(probs_kernel, out, [], *arrays, fetched=True, stored=True, limit=24 << 20)


def value_kernel(tensor_ref, probs_ref, weight_ref, *refs):
    count = 2 * len(CHUNKS)
    whole_refs, last_refs = refs[: -3 - count], refs[-3 - count : -3]
    out_ref, grad_ref, total_ref = refs[-3:]
    length, width = out_ref.shape
    heads = width // HEAD_DIM
    step = probs_ref.shape[1] // heads
    block = whole_refs[0].shape[0]
    order = block_order(tensor_ref[0])

    def through(blocks, first):
        lhs = jnp.concatenate([ref[...] for ref in blocks], axis=0)
        cols = slice(first, first + lhs.shape[1])
        return lax.dot_general(lhs, weight_ref[:, cols], (((1,), (1,)), ((), ())), preferred_element_type=jnp.float32)

    def put(places, total):
        for i, place in enumerate(places):
            rows = pl.ds(pl.multiple_of(order[place] * block, block), block)
            grad_ref[rows, :] = total[i * block : (i + 1) * block].astype(grad_ref.dtype)

    put(range(6), through(whole_refs, 0))
    total = None
    for i, first in enumerate(FIRSTS):
        piece = through(last_refs[2 * i : 2 * i + 2], first)
        total = piece if total is None else total + piece
    put((6, 7), total)

    for head in range(heads):
        cols = slice(head * HEAD_DIM, (head + 1) * HEAD_DIM)
        base = 0
        for first in range(0, length, step):
            stop = first + step
            probs = probs_ref[base : base + stop, head * step : (head + 1) * step]
            base += stop
            update = jnp.dot(probs, grad_ref[first:stop, cols], preferred_element_type=jnp.float32)
            if first == 0:
                total_ref[0:stop, :] = update
            else:
                total_ref[0:first, :] = total_ref[0:first, :] + update[0:first]
                total_ref[first:stop, :] = update[first:stop]
        out_ref[:, cols] = total_ref[...].astype(out_ref.dtype)


def value_rows(tensor, probs, weight, whole, last):
    width = weight.shape[0]
    length = 8 * whole[0].shape[0]
    return local_call(
        value_kernel,
        jax.ShapeDtypeStruct((length, width), jnp.bfloat16),
        [tensor],
        probs,
        weight,
        *whole,
        *last,
        fetched=True,
        stored=True,
        limit=40 << 20,
        scratch=[pltpu.VMEM((length, width), jnp.bfloat16), pltpu.VMEM((length, HEAD_DIM), jnp.float32)],
    )


def sum_kernel(*refs):
    out_ref = refs[-1]
    for first, ref in zip(FIRSTS, refs):
        here = slice(first, first + ref.shape[2])
        total = ref[0].astype(jnp.float32)
        for i in range(1, ref.shape[0]):
            total = total + ref[i].astype(jnp.float32)
        out_ref[:, here] = total.astype(out_ref.dtype)


def sum_slabs(chunks):
    out = like(chunks[0], chunks[0].shape[1], sum(CHUNKS))
    return local_call(sum_kernel, out, [], *chunks)


def send(array, pairs):
    return lax.ppermute(array, "tensor", pairs)


def shards(d_out, attn_out, queries, keys, out_weight, segment_ids):
    return step(d_out[0], attn_out[0], queries[0], keys[0], out_weight, segment_ids[0])


def step(whole, outputs, queries, keys, weight, segments):
    index = lax.axis_index("tensor")
    tensor = index.astype(jnp.int32)[None]
    width = outputs.shape[1]
    rows = width // DP
    count = len(CHUNKS)
    near = send(whole, PAIRS)
    middle_a = send(whole, MIDDLE)
    features = ordered_features(tensor, outputs)
    twin = send(whole, PARTNER)
    parts = split(near)
    ends_a = send(middle_a, ENDS)
    middle_b = [send(parts[i], MIDDLE) for i in range(count)]
    twin_near = send(near, PARTNER)
    probs = probs_columns(queries, keys, segments)
    ends_b = [send(middle_b[i], ENDS) for i in range(count)]
    far_a = pick(tensor, middle_a, ends_a)
    twin_a = send(far_a, PARTNER)
    full = [whole, twin, near, twin_near, far_a, twin_a]
    last, moved = [], []
    for i in range(count):
        far_b = pick(tensor, middle_b[i], ends_b[i])
        twin_b = send(far_b, PARTNER)
        last += [far_b, twin_b]
        product = product_rows(features, full, [far_b, twin_b], FIRSTS[i])
        product = product.reshape(NX, width // NX, CHUNKS[i])
        moved.append(lax.all_to_all(product, "dp", 0, 0, axis_index_groups=GROUPS_X))
    total = sum_slabs(moved).reshape(NY * NZ, rows, whole.shape[1])
    total = lax.all_to_all(total, "dp", 0, 0, axis_index_groups=GROUPS_YZ)
    owned = jnp.sum(total.astype(jnp.float32), axis=0) / DP
    values = value_rows(tensor, probs, weight, full, last)
    return values[None], owned


def solution(mesh):
    placed = (
        P("dp", "tensor", None),
        P("dp", None, "tensor"),
        P("dp", None, "tensor"),
        P("dp", None, "tensor"),
        P("tensor", None),
        P("dp", None),
    )
    return jax.shard_map(
        shards,
        mesh=mesh,
        in_specs=placed,
        out_specs=(P("dp", None, "tensor"), P(("tensor", "dp"), None)),
        check_vma=False,
    )
```

```python
import jax
import jax.numpy as jnp
from jax import lax
from jax.experimental import pallas as pl
from jax.experimental.pallas import tpu as pltpu
from jax.sharding import PartitionSpec as P

HEAD_DIM = 128
NY, NZ, NX = 8, 3, 4
DP = NY * NZ * NX
CHUNKS = (1280, 1280)
FIRSTS = tuple(sum(CHUNKS[:i]) for i in range(len(CHUNKS)))
VMEM_LIMIT = 12 << 20


def dp_at(y, z, x):
    return (y * NZ + z) * NX + x


GROUPS_X = [[dp_at(y, z, x) for x in range(NX)] for y in range(NY) for z in range(NZ)]
GROUPS_YZ = [[dp_at(y, z, x) for y in range(NY) for z in range(NZ)] for x in range(NX)]

PAIRS = [(t, t ^ 2) for t in range(8)]
MIDDLE = [(2, 4), (3, 5), (4, 2), (5, 3)]
ENDS = [(2, 0), (3, 1), (4, 6), (5, 7)]
PARTNER = [(t, t ^ 1) for t in range(8)]

FAR = 2
VMEM = pl.BlockSpec(memory_space=pltpu.VMEM)
SMEM = pl.BlockSpec(memory_space=pltpu.SMEM)


def local_call(
    kernel, out, scalars, *arrays, scratch=(), fetched=False, stored=False, limit=VMEM_LIMIT, column=(), resident=0
):
    def whole(array):
        return pl.BlockSpec(array.shape, lambda i: (0,) * len(array.shape), pipeline_mode=pl.Buffered(1))

    def fetch(i, array):
        if not fetched or i >= len(arrays) - resident:
            return VMEM
        if i not in column:
            return whole(array)
        shape, at = (array.shape[0], out.shape[1]), column[i]
        return pl.BlockSpec(shape, lambda i: (0, at), pipeline_mode=pl.Buffered(1))

    if fetched:
        count = len(arrays) - resident
        arrays = [pltpu.with_memory_space_constraint(a, pltpu.HBM) for a in arrays[:count]] + list(arrays[count:])
    return pl.pallas_call(
        kernel,
        out_shape=pltpu.HBM(out.shape, out.dtype) if stored else out,
        grid=(1,) if fetched or stored else (),
        in_specs=[SMEM] * len(scalars) + [fetch(i, array) for i, array in enumerate(arrays)],
        out_specs=whole(out) if stored else jax.tree.map(lambda _: VMEM, out),
        scratch_shapes=list(scratch),
        compiler_params=pltpu.CompilerParams(vmem_limit_bytes=limit),
    )(*scalars, *arrays)


def like(array, *shape):
    return jax.ShapeDtypeStruct(shape, array.dtype)


def block_order(tensor):
    core = tensor & 1
    low = tensor < 4
    far_a = jnp.where(low, 4, 2) + core
    far_b = jnp.where(low, 6, 0) + core
    near = tensor ^ 2
    return [tensor, tensor ^ 1, near, near ^ 1, far_a, far_b, far_a ^ 1, far_b ^ 1]


def split_kernel(whole_ref, *out_refs):
    for first, ref in zip(FIRSTS, out_refs):
        ref[...] = whole_ref[:, first : first + ref.shape[1]]


def split(whole):
    out = [like(whole, whole.shape[0], c) for c in CHUNKS]
    return local_call(split_kernel, out, [], whole)


def features_kernel(tensor_ref, select_ref, rows_ref, out_ref):
    block = out_ref.shape[1] // 8
    for i, at in enumerate(block_order(tensor_ref[0])):
        rows = rows_ref[pl.ds(pl.multiple_of(at * block, block), block), :]
        out_ref[:, i * block : (i + 1) * block] = lax.dot_general(
            select_ref[...], rows, (((1,), (1,)), ((), ())), preferred_element_type=jnp.float32
        ).astype(out_ref.dtype)


def ordered_features(tensor, outputs):
    length, width = outputs.shape
    rows = width // DP
    new = jnp.arange(width)
    x, y, z, r = new // (width // NX), new // (NZ * rows) % NY, new // rows % NZ, new % rows
    old = dp_at(y, z, x) * rows + r
    select = (old[:, None] == jnp.arange(width)[None, :]).astype(outputs.dtype)
    return local_call(features_kernel, like(outputs, width, length), [tensor], select, outputs, stored=True)


def pick(tensor, middle_a, ends_a, middle_b, ends_b, first):
    block, cols = middle_b.shape
    here = slice(first, first + cols)

    def kernel(tensor_ref, middle_a_ref, ends_a_ref, middle_b_ref, ends_b_ref, out_ref):
        tensor = tensor_ref[0]
        at_end = (tensor < 2) | (tensor >= 6)

        @pl.when(at_end)
        def _():
            out_ref[0:block, :] = ends_a_ref[...]
            out_ref[block:, :] = ends_b_ref[...]

        @pl.when(jnp.logical_not(at_end))
        def _():
            out_ref[0:block, :] = middle_a_ref[:, here]
            out_ref[block:, :] = middle_b_ref[...]

    return local_call(kernel, like(middle_b, 2 * block, cols), [tensor], middle_a, ends_a, middle_b, ends_b)


def product_rows(features, whole, last, first):
    width = features.shape[0]
    cols = last[0].shape[1]

    def kernel(features_ref, *refs):
        out_ref = refs[-1]
        for at in range(0, cols, 256):
            here = slice(at, at + 256)
            blocks = [ref[:, here] for ref in refs[:-1]]
            out_ref[:, here] = jnp.dot(
                features_ref[...], jnp.concatenate(blocks, axis=0), preferred_element_type=jnp.float32
            ).astype(out_ref.dtype)

    out = jax.ShapeDtypeStruct((width, cols), jnp.bfloat16)
    column = {1 + i: first // cols for i in range(len(whole))}
    return local_call(kernel, out, [], features, *whole, *last, fetched=True, stored=True, column=column, resident=FAR)


def probs_kernel(query_ref, key_ref, segment_ref, out_ref):
    length = query_ref.shape[0]
    heads = query_ref.shape[1] // HEAD_DIM
    step = out_ref.shape[1] // heads
    scale = HEAD_DIM**-0.5
    segments = segment_ref[...]
    begin = jnp.zeros_like(segments)
    for id in (0, 1):
        begin = begin + jnp.where(segments > id, jnp.sum((segments == id).astype(jnp.int32), axis=1, keepdims=True), 0)
    base = 0
    for first in range(0, length, step):
        stop = first + step
        key_at = lax.broadcasted_iota(jnp.int32, (stop, step), 0)
        query_at = lax.broadcasted_iota(jnp.int32, (stop, step), 1) + first
        allowed = (key_at <= query_at) & (key_at >= begin[:, first:stop])
        bias = jnp.where(allowed, 0.0, -1e30)
        for head in range(heads):
            cols = slice(head * HEAD_DIM, (head + 1) * HEAD_DIM)
            scores = lax.dot_general(
                key_ref[0:stop, cols],
                query_ref[first:stop, cols],
                (((1,), (1,)), ((), ())),
                preferred_element_type=jnp.float32,
            )
            masked = scores + bias
            highest = jnp.max(masked, axis=0, keepdims=True)
            weights = jnp.exp((masked - highest) * scale)
            inverse = 1.0 / jnp.sum(weights, axis=0, keepdims=True)
            out_ref[base : base + stop, head * step : (head + 1) * step] = (weights * inverse).astype(out_ref.dtype)
        base += stop


def probs_columns(queries, keys, segments):
    length, width = queries.shape
    step = min(256, length)
    spans = sum(range(step, length + 1, step))
    out = like(queries, spans, width // HEAD_DIM * step)
    arrays = (queries, keys, segments[None, :])
    return local_call(probs_kernel, out, [], *arrays, fetched=True, stored=True, limit=24 << 20)


def value_kernel(tensor_ref, probs_ref, weight_ref, *refs):
    count = FAR * len(CHUNKS)
    whole_refs, last_refs = refs[: -3 - count], refs[-3 - count : -3]
    out_ref, grad_ref, total_ref = refs[-3:]
    length, width = out_ref.shape
    heads = width // HEAD_DIM
    step = probs_ref.shape[1] // heads
    block = whole_refs[0].shape[0]
    order = block_order(tensor_ref[0])

    def through(blocks, first):
        lhs = jnp.concatenate([ref[...] for ref in blocks], axis=0)
        cols = slice(first, first + lhs.shape[1])
        return lax.dot_general(lhs, weight_ref[:, cols], (((1,), (1,)), ((), ())), preferred_element_type=jnp.float32)

    def put(places, total):
        for i, place in enumerate(places):
            rows = pl.ds(pl.multiple_of(order[place] * block, block), block)
            grad_ref[rows, :] = total[i * block : (i + 1) * block].astype(grad_ref.dtype)

    put(range(4), through(whole_refs, 0))
    total = None
    for i, first in enumerate(FIRSTS):
        piece = through(last_refs[FAR * i : FAR * i + FAR], first)
        total = piece if total is None else total + piece
    put(range(4, 8), total)

    for head in range(heads):
        cols = slice(head * HEAD_DIM, (head + 1) * HEAD_DIM)
        base = 0
        for first in range(0, length, step):
            stop = first + step
            probs = probs_ref[base : base + stop, head * step : (head + 1) * step]
            base += stop
            update = jnp.dot(probs, grad_ref[first:stop, cols], preferred_element_type=jnp.float32)
            if first == 0:
                total_ref[0:stop, :] = update
            else:
                total_ref[0:first, :] = total_ref[0:first, :] + update[0:first]
                total_ref[first:stop, :] = update[first:stop]
        out_ref[:, cols] = total_ref[...].astype(out_ref.dtype)


def value_rows(tensor, probs, weight, whole, last):
    width = weight.shape[0]
    length = 8 * whole[0].shape[0]
    return local_call(
        value_kernel,
        jax.ShapeDtypeStruct((length, width), jnp.bfloat16),
        [tensor],
        probs,
        weight,
        *whole,
        *last,
        fetched=True,
        stored=True,
        limit=40 << 20,
        scratch=[pltpu.VMEM((length, width), jnp.bfloat16), pltpu.VMEM((length, HEAD_DIM), jnp.float32)],
    )


def sum_kernel(*refs):
    out_ref = refs[-1]
    for first, ref in zip(FIRSTS, refs):
        here = slice(first, first + ref.shape[2])
        total = ref[0].astype(jnp.float32)
        for i in range(1, ref.shape[0]):
            total = total + ref[i].astype(jnp.float32)
        out_ref[:, here] = total.astype(out_ref.dtype)


def sum_slabs(chunks):
    out = like(chunks[0], chunks[0].shape[1], sum(CHUNKS))
    return local_call(sum_kernel, out, [], *chunks)


def send(array, pairs):
    return lax.ppermute(array, "tensor", pairs)


def shards(d_out, attn_out, queries, keys, out_weight, segment_ids):
    return step(d_out[0], attn_out[0], queries[0], keys[0], out_weight, segment_ids[0])


def step(whole, outputs, queries, keys, weight, segments):
    index = lax.axis_index("tensor")
    tensor = index.astype(jnp.int32)[None]
    width = outputs.shape[1]
    rows = width // DP
    count = len(CHUNKS)
    near = send(whole, PAIRS)
    middle_a = send(whole, MIDDLE)
    features = ordered_features(tensor, outputs)
    twin = send(whole, PARTNER)
    probs = probs_columns(queries, keys, segments)
    near_parts = split(near)
    middle_parts = split(middle_a)
    middle_b = [send(near_parts[i], MIDDLE) for i in range(count)]
    ends_a = [send(middle_parts[i], ENDS) for i in range(count)]
    ends_b = [send(middle_b[i], ENDS) for i in range(count)]
    full = [whole, twin, near, send(near, PARTNER)]
    last, moved = [], []
    for i in range(count):
        far = pick(tensor, middle_a, ends_a[i], middle_b[i], ends_b[i], FIRSTS[i])
        pair = [far, send(far, PARTNER)]
        last += pair
        product = product_rows(features, full, pair, FIRSTS[i])
        product = product.reshape(NX, width // NX, CHUNKS[i])
        moved.append(lax.all_to_all(product, "dp", 0, 0, axis_index_groups=GROUPS_X))
    total = sum_slabs(moved).reshape(NY * NZ, rows, whole.shape[1])
    total = lax.all_to_all(total, "dp", 0, 0, axis_index_groups=GROUPS_YZ)
    owned = jnp.sum(total.astype(jnp.float32), axis=0) / DP
    values = value_rows(tensor, probs, weight, full, last)
    return values[None], owned


def solution(mesh):
    placed = (
        P("dp", "tensor", None),
        P("dp", None, "tensor"),
        P("dp", None, "tensor"),
        P("dp", None, "tensor"),
        P("tensor", None),
        P("dp", None),
    )
    return jax.shard_map(
        shards,
        mesh=mesh,
        in_specs=placed,
        out_specs=(P("dp", None, "tensor"), P(("tensor", "dp"), None)),
        check_vma=False,
    )
```

```python
import jax
import jax.numpy as jnp
from jax import lax
from jax.experimental import pallas as pl
from jax.experimental.pallas import tpu as pltpu
from jax.sharding import PartitionSpec as P

HEAD_DIM = 128
NY, NZ, NX = 8, 3, 4
DP = NY * NZ * NX
CHUNKS = (1280, 1280)
FIRSTS = tuple(sum(CHUNKS[:i]) for i in range(len(CHUNKS)))
VMEM_LIMIT = 12 << 20


def dp_at(y, z, x):
    return (y * NZ + z) * NX + x


GROUPS_X = [[dp_at(y, z, x) for x in range(NX)] for y in range(NY) for z in range(NZ)]
GROUPS_YZ = [[dp_at(y, z, x) for y in range(NY) for z in range(NZ)] for x in range(NX)]

PAIRS = [(t, t ^ 2) for t in range(8)]
MIDDLE = [(2, 4), (3, 5), (4, 2), (5, 3)]
ENDS = [(2, 0), (3, 1), (4, 6), (5, 7)]
PARTNER = [(t, t ^ 1) for t in range(8)]

FAR = 2
VMEM = pl.BlockSpec(memory_space=pltpu.VMEM)
SMEM = pl.BlockSpec(memory_space=pltpu.SMEM)


def local_call(
    kernel, out, scalars, *arrays, scratch=(), fetched=False, stored=False, limit=VMEM_LIMIT, column=(), resident=0
):
    def whole(array):
        return pl.BlockSpec(array.shape, lambda i: (0,) * len(array.shape), pipeline_mode=pl.Buffered(1))

    def fetch(i, array):
        if not fetched or i >= len(arrays) - resident:
            return VMEM
        if i not in column:
            return whole(array)
        shape, at = (array.shape[0], out.shape[1]), column[i]
        return pl.BlockSpec(shape, lambda i: (0, at), pipeline_mode=pl.Buffered(1))

    if fetched:
        count = len(arrays) - resident
        arrays = [pltpu.with_memory_space_constraint(a, pltpu.HBM) for a in arrays[:count]] + list(arrays[count:])
    return pl.pallas_call(
        kernel,
        out_shape=pltpu.HBM(out.shape, out.dtype) if stored else out,
        grid=(1,) if fetched or stored else (),
        in_specs=[SMEM] * len(scalars) + [fetch(i, array) for i, array in enumerate(arrays)],
        out_specs=whole(out) if stored else jax.tree.map(lambda _: VMEM, out),
        scratch_shapes=list(scratch),
        compiler_params=pltpu.CompilerParams(vmem_limit_bytes=limit),
    )(*scalars, *arrays)


def like(array, *shape):
    return jax.ShapeDtypeStruct(shape, array.dtype)


def block_order(tensor):
    core = tensor & 1
    low = tensor < 4
    far_a = jnp.where(low, 4, 2) + core
    far_b = jnp.where(low, 6, 0) + core
    near = tensor ^ 2
    return [tensor, tensor ^ 1, near, far_a, far_b, near ^ 1, far_a ^ 1, far_b ^ 1]


def split_kernel(whole_ref, *out_refs):
    for first, ref in zip(FIRSTS, out_refs):
        ref[...] = whole_ref[:, first : first + ref.shape[1]]


def split(whole):
    out = [like(whole, whole.shape[0], c) for c in CHUNKS]
    return local_call(split_kernel, out, [], whole)


def features_kernel(tensor_ref, select_ref, rows_ref, out_ref):
    block = out_ref.shape[1] // 8
    for i, at in enumerate(block_order(tensor_ref[0])):
        rows = rows_ref[pl.ds(pl.multiple_of(at * block, block), block), :]
        out_ref[:, i * block : (i + 1) * block] = lax.dot_general(
            select_ref[...], rows, (((1,), (1,)), ((), ())), preferred_element_type=jnp.float32
        ).astype(out_ref.dtype)


def ordered_features(tensor, outputs):
    length, width = outputs.shape
    rows = width // DP
    new = jnp.arange(width)
    x, y, z, r = new // (width // NX), new // (NZ * rows) % NY, new // rows % NZ, new % rows
    old = dp_at(y, z, x) * rows + r
    select = (old[:, None] == jnp.arange(width)[None, :]).astype(outputs.dtype)
    return local_call(features_kernel, like(outputs, width, length), [tensor], select, outputs, stored=True)


def pick(tensor, near, middle_a, ends_a, middle_b, ends_b, first):
    block, cols = middle_b.shape
    here = slice(first, first + cols)

    def kernel(tensor_ref, near_ref, middle_a_ref, ends_a_ref, middle_b_ref, ends_b_ref, out_ref):
        out_ref[0:block, :] = near_ref[...]
        tensor = tensor_ref[0]
        at_end = (tensor < 2) | (tensor >= 6)

        @pl.when(at_end)
        def _():
            out_ref[block : 2 * block, :] = ends_a_ref[...]
            out_ref[2 * block :, :] = ends_b_ref[...]

        @pl.when(jnp.logical_not(at_end))
        def _():
            out_ref[block : 2 * block, :] = middle_a_ref[:, here]
            out_ref[2 * block :, :] = middle_b_ref[...]

    arrays = (near, middle_a, ends_a, middle_b, ends_b)
    return local_call(kernel, like(middle_b, 3 * block, cols), [tensor], *arrays)


def product_rows(features, whole, last, first):
    width = features.shape[0]
    cols = last[0].shape[1]

    def kernel(features_ref, *refs):
        out_ref = refs[-1]
        for at in range(0, cols, 256):
            here = slice(at, at + 256)
            blocks = [ref[:, here] for ref in refs[:-1]]
            out_ref[:, here] = jnp.dot(
                features_ref[...], jnp.concatenate(blocks, axis=0), preferred_element_type=jnp.float32
            ).astype(out_ref.dtype)

    out = jax.ShapeDtypeStruct((width, cols), jnp.bfloat16)
    column = {1 + i: first // cols for i in range(len(whole))}
    return local_call(kernel, out, [], features, *whole, *last, fetched=True, stored=True, column=column, resident=FAR)


def value_kernel(tensor_ref, query_ref, key_ref, segment_ref, weight_ref, *refs):
    count = FAR * len(CHUNKS)
    whole_refs, last_refs = refs[: -3 - count], refs[-3 - count : -3]
    out_ref, grad_ref, total_ref = refs[-3:]
    length, width = out_ref.shape
    heads = width // HEAD_DIM
    step = min(256, length)
    block = whole_refs[0].shape[0]
    order = block_order(tensor_ref[0])

    def through(blocks, first):
        lhs = jnp.concatenate([ref[...] for ref in blocks], axis=0)
        cols = slice(first, first + lhs.shape[1])
        return lax.dot_general(lhs, weight_ref[:, cols], (((1,), (1,)), ((), ())), preferred_element_type=jnp.float32)

    def put(places, total):
        for i, place in enumerate(places):
            rows = pl.ds(pl.multiple_of(order[place] * block, block), block)
            grad_ref[rows, :] = total[i * block : (i + 1) * block].astype(grad_ref.dtype)

    put(range(2), through(whole_refs, 0))
    total = None
    for i, first in enumerate(FIRSTS):
        piece = through(last_refs[FAR * i : FAR * i + FAR], first)
        total = piece if total is None else total + piece
    put(range(2, 8), total)

    segments = segment_ref[...]
    begin = jnp.zeros_like(segments)
    for id in (0, 1):
        begin = begin + jnp.where(segments > id, jnp.sum((segments == id).astype(jnp.int32), axis=1, keepdims=True), 0)
    scale = HEAD_DIM**-0.5
    for first in range(0, length, step):
        stop = first + step
        key_at = lax.broadcasted_iota(jnp.int32, (stop, step), 0)
        query_at = lax.broadcasted_iota(jnp.int32, (stop, step), 1) + first
        allowed = (key_at <= query_at) & (key_at >= begin[:, first:stop])
        bias = jnp.where(allowed, 0.0, -1e30)
        for head in range(heads):
            cols = slice(head * HEAD_DIM, (head + 1) * HEAD_DIM)
            scores = lax.dot_general(
                key_ref[0:stop, cols],
                query_ref[first:stop, cols],
                (((1,), (1,)), ((), ())),
                preferred_element_type=jnp.float32,
            )
            masked = scores + bias
            highest = jnp.max(masked, axis=0, keepdims=True)
            weights = jnp.exp((masked - highest) * scale)
            inverse = 1.0 / jnp.sum(weights, axis=0, keepdims=True)
            probs = (weights * inverse).astype(grad_ref.dtype)
            update = jnp.dot(probs, grad_ref[first:stop, cols], preferred_element_type=jnp.float32)
            if first > 0:
                total_ref[0:first, cols] = total_ref[0:first, cols] + update[0:first]
            total_ref[first:stop, cols] = update[first:stop]
    out_ref[...] = total_ref[...].astype(out_ref.dtype)


def value_rows(tensor, queries, keys, segments, weight, whole, last):
    length, width = queries.shape
    return local_call(
        value_kernel,
        like(queries, length, width),
        [tensor],
        queries,
        keys,
        segments[None, :],
        weight,
        *whole,
        *last,
        fetched=True,
        stored=True,
        limit=40 << 20,
        scratch=[pltpu.VMEM((length, width), jnp.bfloat16), pltpu.VMEM((length, width), jnp.float32)],
    )


def sum_kernel(*refs):
    out_ref = refs[-1]
    for first, ref in zip(FIRSTS, refs):
        here = slice(first, first + ref.shape[2])
        total = ref[0].astype(jnp.float32)
        for i in range(1, ref.shape[0]):
            total = total + ref[i].astype(jnp.float32)
        out_ref[:, here] = total.astype(out_ref.dtype)


def sum_slabs(chunks):
    out = like(chunks[0], chunks[0].shape[1], sum(CHUNKS))
    return local_call(sum_kernel, out, [], *chunks)


def send(array, pairs):
    return lax.ppermute(array, "tensor", pairs)


def shards(d_out, attn_out, queries, keys, out_weight, segment_ids):
    return step(d_out[0], attn_out[0], queries[0], keys[0], out_weight, segment_ids[0])


def step(whole, outputs, queries, keys, weight, segments):
    index = lax.axis_index("tensor")
    tensor = index.astype(jnp.int32)[None]
    width = outputs.shape[1]
    rows = width // DP
    count = len(CHUNKS)
    own_parts = split(whole)
    near = [send(own_parts[i], PAIRS) for i in range(count)]
    middle_a = send(whole, MIDDLE)
    features = ordered_features(tensor, outputs)
    full = [whole, send(whole, PARTNER)]
    middle_parts = split(middle_a)
    middle_b = [send(near[i], MIDDLE) for i in range(count)]
    ends_a = [send(middle_parts[i], ENDS) for i in range(count)]
    ends_b = [send(middle_b[i], ENDS) for i in range(count)]
    last, moved = [], []
    for i in range(count):
        got = pick(tensor, near[i], middle_a, ends_a[i], middle_b[i], ends_b[i], FIRSTS[i])
        pair = [got, send(got, PARTNER)]
        last += pair
        product = product_rows(features, full, pair, FIRSTS[i])
        product = product.reshape(NX, width // NX, CHUNKS[i])
        moved.append(lax.all_to_all(product, "dp", 0, 0, axis_index_groups=GROUPS_X))
    total = sum_slabs(moved).reshape(NY * NZ, rows, whole.shape[1])
    total = lax.all_to_all(total, "dp", 0, 0, axis_index_groups=GROUPS_YZ)
    owned = jnp.sum(total.astype(jnp.float32), axis=0) / DP
    values = value_rows(tensor, queries, keys, segments, weight, full, last)
    return values[None], owned


def solution(mesh):
    placed = (
        P("dp", "tensor", None),
        P("dp", None, "tensor"),
        P("dp", None, "tensor"),
        P("dp", None, "tensor"),
        P("tensor", None),
        P("dp", None),
    )
    return jax.shard_map(
        shards,
        mesh=mesh,
        in_specs=placed,
        out_specs=(P("dp", None, "tensor"), P(("tensor", "dp"), None)),
        check_vma=False,
    )
```

```python
import jax
import jax.numpy as jnp
from jax import lax
from jax.experimental import pallas as pl
from jax.experimental.pallas import tpu as pltpu
from jax.sharding import PartitionSpec as P

HEAD_DIM = 128
NY, NZ, NX = 8, 3, 4
DP = NY * NZ * NX
CHUNKS = (1280, 1280)
FIRSTS = tuple(sum(CHUNKS[:i]) for i in range(len(CHUNKS)))
VMEM_LIMIT = 12 << 20


def dp_at(y, z, x):
    return (y * NZ + z) * NX + x


GROUPS_X = [[dp_at(y, z, x) for x in range(NX)] for y in range(NY) for z in range(NZ)]
GROUPS_YZ = [[dp_at(y, z, x) for y in range(NY) for z in range(NZ)] for x in range(NX)]

PAIRS = [(t, t ^ 2) for t in range(8)]
MIDDLE = [(2, 4), (3, 5), (4, 2), (5, 3)]
ENDS = [(2, 0), (3, 1), (4, 6), (5, 7)]
PARTNER = [(t, t ^ 1) for t in range(8)]

FAR = 2
VMEM = pl.BlockSpec(memory_space=pltpu.VMEM)
SMEM = pl.BlockSpec(memory_space=pltpu.SMEM)


def local_call(
    kernel, out, scalars, *arrays, scratch=(), fetched=False, stored=False, limit=VMEM_LIMIT, column=(), resident=0
):
    def whole(array):
        return pl.BlockSpec(array.shape, lambda i: (0,) * len(array.shape), pipeline_mode=pl.Buffered(1))

    def fetch(i, array):
        if not fetched or i >= len(arrays) - resident:
            return VMEM
        if i not in column:
            return whole(array)
        shape, at = (array.shape[0], out.shape[1]), column[i]
        return pl.BlockSpec(shape, lambda i: (0, at), pipeline_mode=pl.Buffered(1))

    if fetched:
        count = len(arrays) - resident
        arrays = [pltpu.with_memory_space_constraint(a, pltpu.HBM) for a in arrays[:count]] + list(arrays[count:])
    return pl.pallas_call(
        kernel,
        out_shape=pltpu.HBM(out.shape, out.dtype) if stored else out,
        grid=(1,) if fetched or stored else (),
        in_specs=[SMEM] * len(scalars) + [fetch(i, array) for i, array in enumerate(arrays)],
        out_specs=whole(out) if stored else jax.tree.map(lambda _: VMEM, out),
        scratch_shapes=list(scratch),
        compiler_params=pltpu.CompilerParams(vmem_limit_bytes=limit),
    )(*scalars, *arrays)


def like(array, *shape):
    return jax.ShapeDtypeStruct(shape, array.dtype)


def block_order(tensor):
    core = tensor & 1
    low = tensor < 4
    far_a = jnp.where(low, 4, 2) + core
    far_b = jnp.where(low, 6, 0) + core
    near = tensor ^ 2
    return [tensor, tensor ^ 1, near, far_a, far_b, near ^ 1, far_a ^ 1, far_b ^ 1]


def split_kernel(whole_ref, *out_refs):
    for first, ref in zip(FIRSTS, out_refs):
        ref[...] = whole_ref[:, first : first + ref.shape[1]]


def split(whole):
    out = [like(whole, whole.shape[0], c) for c in CHUNKS]
    return local_call(split_kernel, out, [], whole)


def features_kernel(tensor_ref, select_ref, rows_ref, out_ref):
    block = out_ref.shape[1] // 8
    for i, at in enumerate(block_order(tensor_ref[0])):
        rows = rows_ref[pl.ds(pl.multiple_of(at * block, block), block), :]
        out_ref[:, i * block : (i + 1) * block] = lax.dot_general(
            select_ref[...], rows, (((1,), (1,)), ((), ())), preferred_element_type=jnp.float32
        ).astype(out_ref.dtype)


def ordered_features(tensor, outputs):
    length, width = outputs.shape
    rows = width // DP
    new = jnp.arange(width)
    x, y, z, r = new // (width // NX), new // (NZ * rows) % NY, new // rows % NZ, new % rows
    old = dp_at(y, z, x) * rows + r
    select = (old[:, None] == jnp.arange(width)[None, :]).astype(outputs.dtype)
    return local_call(features_kernel, like(outputs, width, length), [tensor], select, outputs, stored=True)


def pick(tensor, near, middle_a, ends_a, middle_b, ends_b):
    block, cols = middle_b.shape

    def kernel(tensor_ref, near_ref, middle_a_ref, ends_a_ref, middle_b_ref, ends_b_ref, out_ref):
        out_ref[0:block, :] = near_ref[...]
        tensor = tensor_ref[0]
        at_end = (tensor < 2) | (tensor >= 6)

        @pl.when(at_end)
        def _():
            out_ref[block : 2 * block, :] = ends_a_ref[...]
            out_ref[2 * block :, :] = ends_b_ref[...]

        @pl.when(jnp.logical_not(at_end))
        def _():
            out_ref[block : 2 * block, :] = middle_a_ref[...]
            out_ref[2 * block :, :] = middle_b_ref[...]

    arrays = (near, middle_a, ends_a, middle_b, ends_b)
    return local_call(kernel, like(middle_b, 3 * block, cols), [tensor], *arrays)


def product_rows(features, whole, last, first):
    width = features.shape[0]
    cols = last[0].shape[1]

    def kernel(features_ref, *refs):
        out_ref = refs[-1]
        for at in range(0, cols, 256):
            here = slice(at, at + 256)
            blocks = [ref[:, here] for ref in refs[:-1]]
            out_ref[:, here] = jnp.dot(
                features_ref[...], jnp.concatenate(blocks, axis=0), preferred_element_type=jnp.float32
            ).astype(out_ref.dtype)

    out = jax.ShapeDtypeStruct((width, cols), jnp.bfloat16)
    column = {1 + i: first // cols for i in range(len(whole))}
    return local_call(kernel, out, [], features, *whole, *last, fetched=True, stored=True, column=column, resident=FAR)


def value_kernel(tensor_ref, query_ref, key_ref, segment_ref, weight_ref, *refs):
    count = FAR * len(CHUNKS)
    whole_refs, last_refs = refs[: -3 - count], refs[-3 - count : -3]
    out_ref, grad_ref, total_ref = refs[-3:]
    length, width = out_ref.shape
    heads = width // HEAD_DIM
    step = min(256, length)
    block = whole_refs[0].shape[0]
    order = block_order(tensor_ref[0])

    def through(blocks, first):
        lhs = jnp.concatenate([ref[...] for ref in blocks], axis=0)
        cols = slice(first, first + lhs.shape[1])
        return lax.dot_general(lhs, weight_ref[:, cols], (((1,), (1,)), ((), ())), preferred_element_type=jnp.float32)

    def put(places, total):
        for i, place in enumerate(places):
            rows = pl.ds(pl.multiple_of(order[place] * block, block), block)
            grad_ref[rows, :] = total[i * block : (i + 1) * block].astype(grad_ref.dtype)

    put(range(2), through(whole_refs, 0))
    total = None
    for i, first in enumerate(FIRSTS):
        piece = through(last_refs[FAR * i : FAR * i + FAR], first)
        total = piece if total is None else total + piece
    put(range(2, 8), total)

    segments = segment_ref[...]
    begin = jnp.zeros_like(segments)
    for id in (0, 1):
        begin = begin + jnp.where(segments > id, jnp.sum((segments == id).astype(jnp.int32), axis=1, keepdims=True), 0)
    scale = HEAD_DIM**-0.5
    for first in range(0, length, step):
        stop = first + step
        key_at = lax.broadcasted_iota(jnp.int32, (stop, step), 0)
        query_at = lax.broadcasted_iota(jnp.int32, (stop, step), 1) + first
        allowed = (key_at <= query_at) & (key_at >= begin[:, first:stop])
        bias = jnp.where(allowed, 0.0, -1e30)
        for head in range(heads):
            cols = slice(head * HEAD_DIM, (head + 1) * HEAD_DIM)
            scores = lax.dot_general(
                key_ref[0:stop, cols],
                query_ref[first:stop, cols],
                (((1,), (1,)), ((), ())),
                preferred_element_type=jnp.float32,
            )
            masked = scores + bias
            highest = jnp.max(masked, axis=0, keepdims=True)
            weights = jnp.exp((masked - highest) * scale)
            inverse = 1.0 / jnp.sum(weights, axis=0, keepdims=True)
            probs = (weights * inverse).astype(grad_ref.dtype)
            update = jnp.dot(probs, grad_ref[first:stop, cols], preferred_element_type=jnp.float32)
            if first > 0:
                total_ref[0:first, cols] = total_ref[0:first, cols] + update[0:first]
            total_ref[first:stop, cols] = update[first:stop]
    out_ref[...] = total_ref[...].astype(out_ref.dtype)


def value_rows(tensor, queries, keys, segments, weight, whole, last):
    length, width = queries.shape
    return local_call(
        value_kernel,
        like(queries, length, width),
        [tensor],
        queries,
        keys,
        segments[None, :],
        weight,
        *whole,
        *last,
        fetched=True,
        stored=True,
        limit=40 << 20,
        scratch=[pltpu.VMEM((length, width), jnp.bfloat16), pltpu.VMEM((length, width), jnp.float32)],
    )


def sum_kernel(*refs):
    out_ref = refs[-1]
    for first, ref in zip(FIRSTS, refs):
        here = slice(first, first + ref.shape[2])
        total = ref[0].astype(jnp.float32)
        for i in range(1, ref.shape[0]):
            total = total + ref[i].astype(jnp.float32)
        out_ref[:, here] = total.astype(out_ref.dtype)


def sum_slabs(chunks):
    out = like(chunks[0], chunks[0].shape[1], sum(CHUNKS))
    return local_call(sum_kernel, out, [], *chunks)


def send(array, pairs):
    return lax.ppermute(array, "tensor", pairs)


def shards(d_out, attn_out, queries, keys, out_weight, segment_ids):
    return step(d_out[0], attn_out[0], queries[0], keys[0], out_weight, segment_ids[0])


def step(whole, outputs, queries, keys, weight, segments):
    index = lax.axis_index("tensor")
    tensor = index.astype(jnp.int32)[None]
    width = outputs.shape[1]
    rows = width // DP
    count = len(CHUNKS)
    own_parts = split(whole)
    near = [send(own_parts[i], PAIRS) for i in range(count)]
    middle_a = [send(own_parts[i], MIDDLE) for i in range(count)]
    features = ordered_features(tensor, outputs)
    full = [whole, send(whole, PARTNER)]
    middle_b = [send(near[i], MIDDLE) for i in range(count)]
    ends_a = [send(middle_a[i], ENDS) for i in range(count)]
    ends_b = [send(middle_b[i], ENDS) for i in range(count)]
    last, moved = [], []
    for i in range(count):
        got = pick(tensor, near[i], middle_a[i], ends_a[i], middle_b[i], ends_b[i])
        pair = [got, send(got, PARTNER)]
        last += pair
        product = product_rows(features, full, pair, FIRSTS[i])
        product = product.reshape(NX, width // NX, CHUNKS[i])
        moved.append(lax.all_to_all(product, "dp", 0, 0, axis_index_groups=GROUPS_X))
    total = sum_slabs(moved).reshape(NY * NZ, rows, whole.shape[1])
    total = lax.all_to_all(total, "dp", 0, 0, axis_index_groups=GROUPS_YZ)
    owned = jnp.sum(total.astype(jnp.float32), axis=0) / DP
    values = value_rows(tensor, queries, keys, segments, weight, full, last)
    return values[None], owned


def solution(mesh):
    placed = (
        P("dp", "tensor", None),
        P("dp", None, "tensor"),
        P("dp", None, "tensor"),
        P("dp", None, "tensor"),
        P("tensor", None),
        P("dp", None),
    )
    return jax.shard_map(
        shards,
        mesh=mesh,
        in_specs=placed,
        out_specs=(P("dp", None, "tensor"), P(("tensor", "dp"), None)),
        check_vma=False,
    )
```

```python
import jax
import jax.numpy as jnp
from jax import lax
from jax.experimental import pallas as pl
from jax.experimental.pallas import tpu as pltpu
from jax.sharding import PartitionSpec as P

HEAD_DIM = 128
NY, NZ, NX = 8, 3, 4
DP = NY * NZ * NX
CHUNKS = (1280, 1280)
FIRSTS = tuple(sum(CHUNKS[:i]) for i in range(len(CHUNKS)))
VMEM_LIMIT = 12 << 20


def dp_at(y, z, x):
    return (y * NZ + z) * NX + x


GROUPS_X = [[dp_at(y, z, x) for x in range(NX)] for y in range(NY) for z in range(NZ)]
GROUPS_YZ = [[dp_at(y, z, x) for y in range(NY) for z in range(NZ)] for x in range(NX)]

PAIRS = [(t, t ^ 2) for t in range(8)]
MIDDLE = [(2, 4), (3, 5), (4, 2), (5, 3)]
ENDS = [(2, 0), (3, 1), (4, 6), (5, 7)]
PARTNER = [(t, t ^ 1) for t in range(8)]

FAR = 2
VMEM = pl.BlockSpec(memory_space=pltpu.VMEM)
SMEM = pl.BlockSpec(memory_space=pltpu.SMEM)


def local_call(
    kernel, out, scalars, *arrays, scratch=(), fetched=False, stored=False, limit=VMEM_LIMIT, column=(), resident=0
):
    def whole(array):
        return pl.BlockSpec(array.shape, lambda i: (0,) * len(array.shape), pipeline_mode=pl.Buffered(1))

    def fetch(i, array):
        if not fetched or i >= len(arrays) - resident:
            return VMEM
        if i not in column:
            return whole(array)
        shape, at = (array.shape[0], out.shape[1]), column[i]
        return pl.BlockSpec(shape, lambda i: (0, at), pipeline_mode=pl.Buffered(1))

    if fetched:
        count = len(arrays) - resident
        arrays = [pltpu.with_memory_space_constraint(a, pltpu.HBM) for a in arrays[:count]] + list(arrays[count:])
    return pl.pallas_call(
        kernel,
        out_shape=pltpu.HBM(out.shape, out.dtype) if stored else out,
        grid=(1,) if fetched or stored else (),
        in_specs=[SMEM] * len(scalars) + [fetch(i, array) for i, array in enumerate(arrays)],
        out_specs=whole(out) if stored else jax.tree.map(lambda _: VMEM, out),
        scratch_shapes=list(scratch),
        compiler_params=pltpu.CompilerParams(vmem_limit_bytes=limit),
    )(*scalars, *arrays)


def like(array, *shape):
    return jax.ShapeDtypeStruct(shape, array.dtype)


def block_order(tensor):
    core = tensor & 1
    low = tensor < 4
    far_a = jnp.where(low, 4, 2) + core
    far_b = jnp.where(low, 6, 0) + core
    near = tensor ^ 2
    return [tensor, tensor ^ 1, near, far_a, far_b, near ^ 1, far_a ^ 1, far_b ^ 1]


def split_kernel(whole_ref, *out_refs):
    for first, ref in zip(FIRSTS, out_refs):
        ref[...] = whole_ref[:, first : first + ref.shape[1]]


def split(whole):
    out = [like(whole, whole.shape[0], c) for c in CHUNKS]
    return local_call(split_kernel, out, [], whole)


def features_kernel(tensor_ref, select_ref, rows_ref, out_ref):
    block = out_ref.shape[1] // 8
    for i, at in enumerate(block_order(tensor_ref[0])):
        rows = rows_ref[pl.ds(pl.multiple_of(at * block, block), block), :]
        out_ref[:, i * block : (i + 1) * block] = lax.dot_general(
            select_ref[...], rows, (((1,), (1,)), ((), ())), preferred_element_type=jnp.float32
        ).astype(out_ref.dtype)


def ordered_features(tensor, outputs):
    length, width = outputs.shape
    rows = width // DP
    new = jnp.arange(width)
    x, y, z, r = new // (width // NX), new // (NZ * rows) % NY, new // rows % NZ, new % rows
    old = dp_at(y, z, x) * rows + r
    select = (old[:, None] == jnp.arange(width)[None, :]).astype(outputs.dtype)
    return local_call(features_kernel, like(outputs, width, length), [tensor], select, outputs)


def pick(tensor, near, middle_a, ends_a, middle_b, ends_b):
    block, cols = middle_b.shape

    def kernel(tensor_ref, near_ref, middle_a_ref, ends_a_ref, middle_b_ref, ends_b_ref, out_ref):
        out_ref[0:block, :] = near_ref[...]
        tensor = tensor_ref[0]
        at_end = (tensor < 2) | (tensor >= 6)

        @pl.when(at_end)
        def _():
            out_ref[block : 2 * block, :] = ends_a_ref[...]
            out_ref[2 * block :, :] = ends_b_ref[...]

        @pl.when(jnp.logical_not(at_end))
        def _():
            out_ref[block : 2 * block, :] = middle_a_ref[...]
            out_ref[2 * block :, :] = middle_b_ref[...]

    arrays = (near, middle_a, ends_a, middle_b, ends_b)
    return local_call(kernel, like(middle_b, 3 * block, cols), [tensor], *arrays)


def product_rows(features, whole, last, first):
    width = features.shape[0]
    cols = last[0].shape[1]

    def kernel(*refs):
        features_ref, out_ref = refs[-2:]
        for at in range(0, cols, 256):
            here = slice(at, at + 256)
            blocks = [ref[:, here] for ref in refs[:-2]]
            out_ref[:, here] = jnp.dot(
                features_ref[...], jnp.concatenate(blocks, axis=0), preferred_element_type=jnp.float32
            ).astype(out_ref.dtype)

    out = jax.ShapeDtypeStruct((width, cols), jnp.bfloat16)
    column = {i: first // cols for i in range(len(whole))}
    arrays = (*whole, *last, features)
    return local_call(kernel, out, [], *arrays, fetched=True, stored=True, column=column, resident=FAR + 1)


def value_kernel(tensor_ref, query_ref, key_ref, segment_ref, weight_ref, *refs):
    count = FAR * len(CHUNKS)
    whole_refs, last_refs = refs[: -3 - count], refs[-3 - count : -3]
    out_ref, grad_ref, total_ref = refs[-3:]
    length, width = out_ref.shape
    heads = width // HEAD_DIM
    step = min(256, length)
    block = whole_refs[0].shape[0]
    order = block_order(tensor_ref[0])

    def through(blocks, first):
        lhs = jnp.concatenate([ref[...] for ref in blocks], axis=0)
        cols = slice(first, first + lhs.shape[1])
        return lax.dot_general(lhs, weight_ref[:, cols], (((1,), (1,)), ((), ())), preferred_element_type=jnp.float32)

    def put(places, total):
        for i, place in enumerate(places):
            rows = pl.ds(pl.multiple_of(order[place] * block, block), block)
            grad_ref[rows, :] = total[i * block : (i + 1) * block].astype(grad_ref.dtype)

    put(range(2), through(whole_refs, 0))
    total = None
    for i, first in enumerate(FIRSTS):
        piece = through(last_refs[FAR * i : FAR * i + FAR], first)
        total = piece if total is None else total + piece
    put(range(2, 8), total)

    segments = segment_ref[...]
    begin = jnp.zeros_like(segments)
    for id in (0, 1):
        begin = begin + jnp.where(segments > id, jnp.sum((segments == id).astype(jnp.int32), axis=1, keepdims=True), 0)
    scale = HEAD_DIM**-0.5
    for first in range(0, length, step):
        stop = first + step
        key_at = lax.broadcasted_iota(jnp.int32, (stop, step), 0)
        query_at = lax.broadcasted_iota(jnp.int32, (stop, step), 1) + first
        allowed = (key_at <= query_at) & (key_at >= begin[:, first:stop])
        bias = jnp.where(allowed, 0.0, -1e30)
        for head in range(heads):
            cols = slice(head * HEAD_DIM, (head + 1) * HEAD_DIM)
            scores = lax.dot_general(
                key_ref[0:stop, cols],
                query_ref[first:stop, cols],
                (((1,), (1,)), ((), ())),
                preferred_element_type=jnp.float32,
            )
            masked = scores + bias
            highest = jnp.max(masked, axis=0, keepdims=True)
            weights = jnp.exp((masked - highest) * scale)
            inverse = 1.0 / jnp.sum(weights, axis=0, keepdims=True)
            probs = (weights * inverse).astype(grad_ref.dtype)
            update = jnp.dot(probs, grad_ref[first:stop, cols], preferred_element_type=jnp.float32)
            if first > 0:
                total_ref[0:first, cols] = total_ref[0:first, cols] + update[0:first]
            total_ref[first:stop, cols] = update[first:stop]
    out_ref[...] = total_ref[...].astype(out_ref.dtype)


def value_rows(tensor, queries, keys, segments, weight, whole, last):
    length, width = queries.shape
    return local_call(
        value_kernel,
        like(queries, length, width),
        [tensor],
        queries,
        keys,
        segments[None, :],
        weight,
        *whole,
        *last,
        fetched=True,
        stored=True,
        limit=40 << 20,
        scratch=[pltpu.VMEM((length, width), jnp.bfloat16), pltpu.VMEM((length, width), jnp.float32)],
    )


def sum_kernel(*refs):
    out_ref = refs[-1]
    for first, ref in zip(FIRSTS, refs):
        here = slice(first, first + ref.shape[2])
        total = ref[0].astype(jnp.float32)
        for i in range(1, ref.shape[0]):
            total = total + ref[i].astype(jnp.float32)
        total = total.astype(out_ref.dtype)
        rows = out_ref.shape[1]
        for owner in range(out_ref.shape[0]):
            out_ref[owner, :, here] = total[owner * rows : (owner + 1) * rows]


def sum_slabs(chunks, rows):
    out = like(chunks[0], chunks[0].shape[1] // rows, rows, sum(CHUNKS))
    return local_call(sum_kernel, out, [], *chunks)


def send(array, pairs):
    return lax.ppermute(array, "tensor", pairs)


def shards(d_out, attn_out, queries, keys, out_weight, segment_ids):
    return step(d_out[0], attn_out[0], queries[0], keys[0], out_weight, segment_ids[0])


def step(whole, outputs, queries, keys, weight, segments):
    index = lax.axis_index("tensor")
    tensor = index.astype(jnp.int32)[None]
    width = outputs.shape[1]
    rows = width // DP
    count = len(CHUNKS)
    own_parts = split(whole)
    near = [send(own_parts[i], PAIRS) for i in range(count)]
    middle_a = [send(own_parts[i], MIDDLE) for i in range(count)]
    features = ordered_features(tensor, outputs)
    full = [whole, send(whole, PARTNER)]
    middle_b = [send(near[i], MIDDLE) for i in range(count)]
    ends_a = [send(middle_a[i], ENDS) for i in range(count)]
    ends_b = [send(middle_b[i], ENDS) for i in range(count)]
    last, moved = [], []
    for i in range(count):
        got = pick(tensor, near[i], middle_a[i], ends_a[i], middle_b[i], ends_b[i])
        pair = [got, send(got, PARTNER)]
        last += pair
        product = product_rows(features, full, pair, FIRSTS[i])
        product = product.reshape(NX, width // NX, CHUNKS[i])
        moved.append(lax.all_to_all(product, "dp", 0, 0, axis_index_groups=GROUPS_X))
    total = sum_slabs(moved, rows)
    total = lax.all_to_all(total, "dp", 0, 0, axis_index_groups=GROUPS_YZ)
    owned = jnp.sum(total.astype(jnp.float32) * (1 / DP), axis=0)
    values = value_rows(tensor, queries, keys, segments, weight, full, last)
    return values[None], owned


def solution(mesh):
    placed = (
        P("dp", "tensor", None),
        P("dp", None, "tensor"),
        P("dp", None, "tensor"),
        P("dp", None, "tensor"),
        P("tensor", None),
        P("dp", None),
    )
    return jax.shard_map(
        shards,
        mesh=mesh,
        in_specs=placed,
        out_specs=(P("dp", None, "tensor"), P(("tensor", "dp"), None)),
        check_vma=False,
    )
```

```python
import jax
import jax.numpy as jnp
from jax import lax
from jax.experimental import pallas as pl
from jax.experimental.pallas import tpu as pltpu
from jax.sharding import PartitionSpec as P

HEAD_DIM = 128
NY, NZ, NX = 8, 3, 4
DP = NY * NZ * NX
CHUNKS = (1280, 1280)
FIRSTS = tuple(sum(CHUNKS[:i]) for i in range(len(CHUNKS)))
VMEM_LIMIT = 12 << 20


def dp_at(y, z, x):
    return (y * NZ + z) * NX + x


GROUPS_X = [[dp_at(y, z, x) for x in range(NX)] for y in range(NY) for z in range(NZ)]
GROUPS_YZ = [[dp_at(y, z, x) for y in range(NY) for z in range(NZ)] for x in range(NX)]

PAIRS = [(t, t ^ 2) for t in range(8)]
MIDDLE = [(2, 4), (3, 5), (4, 2), (5, 3)]
ENDS = [(2, 0), (3, 1), (4, 6), (5, 7)]
PARTNER = [(t, t ^ 1) for t in range(8)]

FAR = 2
VMEM = pl.BlockSpec(memory_space=pltpu.VMEM)
SMEM = pl.BlockSpec(memory_space=pltpu.SMEM)


def local_call(
    kernel, out, scalars, *arrays, scratch=(), fetched=False, stored=False, limit=VMEM_LIMIT, column=(), resident=0
):
    def whole(array):
        return pl.BlockSpec(array.shape, lambda i: (0,) * len(array.shape), pipeline_mode=pl.Buffered(1))

    def fetch(i, array):
        if not fetched or i >= len(arrays) - resident:
            return VMEM
        if i not in column:
            return whole(array)
        shape, at = (array.shape[0], out.shape[1]), column[i]
        return pl.BlockSpec(shape, lambda i: (0, at), pipeline_mode=pl.Buffered(1))

    if fetched:
        count = len(arrays) - resident
        arrays = [pltpu.with_memory_space_constraint(a, pltpu.HBM) for a in arrays[:count]] + list(arrays[count:])
    return pl.pallas_call(
        kernel,
        out_shape=pltpu.HBM(out.shape, out.dtype) if stored else out,
        grid=(1,) if fetched or stored else (),
        in_specs=[SMEM] * len(scalars) + [fetch(i, array) for i, array in enumerate(arrays)],
        out_specs=whole(out) if stored else jax.tree.map(lambda _: VMEM, out),
        scratch_shapes=list(scratch),
        compiler_params=pltpu.CompilerParams(vmem_limit_bytes=limit),
    )(*scalars, *arrays)


def like(array, *shape):
    return jax.ShapeDtypeStruct(shape, array.dtype)


def block_order(tensor):
    core = tensor & 1
    low = tensor < 4
    far_a = jnp.where(low, 4, 2) + core
    far_b = jnp.where(low, 6, 0) + core
    near = tensor ^ 2
    return [tensor, tensor ^ 1, near, far_a, far_b, near ^ 1, far_a ^ 1, far_b ^ 1]


def split_kernel(whole_ref, *out_refs):
    for first, ref in zip(FIRSTS, out_refs):
        ref[...] = whole_ref[:, first : first + ref.shape[1]]


def split(whole):
    out = [like(whole, whole.shape[0], c) for c in CHUNKS]
    return local_call(split_kernel, out, [], whole)


def features_kernel(tensor_ref, select_ref, rows_ref, out_ref):
    block = out_ref.shape[1] // 8
    for i, at in enumerate(block_order(tensor_ref[0])):
        rows = rows_ref[pl.ds(pl.multiple_of(at * block, block), block), :]
        out_ref[:, i * block : (i + 1) * block] = lax.dot_general(
            select_ref[...], rows, (((1,), (1,)), ((), ())), preferred_element_type=jnp.float32
        ).astype(out_ref.dtype)


def ordered_features(tensor, outputs):
    length, width = outputs.shape
    rows = width // DP
    new = jnp.arange(width)
    x, y, z, r = new // (width // NX), new // (NZ * rows) % NY, new // rows % NZ, new % rows
    old = dp_at(y, z, x) * rows + r
    select = (old[:, None] == jnp.arange(width)[None, :]).astype(outputs.dtype)
    return local_call(features_kernel, like(outputs, width, length), [tensor], select, outputs)


def pick(tensor, near, middle_a, ends_a, middle_b, ends_b):
    block, cols = middle_b.shape

    def kernel(tensor_ref, near_ref, middle_a_ref, ends_a_ref, middle_b_ref, ends_b_ref, out_ref):
        out_ref[0:block, :] = near_ref[...]
        tensor = tensor_ref[0]
        at_end = (tensor < 2) | (tensor >= 6)

        @pl.when(at_end)
        def _():
            out_ref[block : 2 * block, :] = ends_a_ref[...]
            out_ref[2 * block :, :] = ends_b_ref[...]

        @pl.when(jnp.logical_not(at_end))
        def _():
            out_ref[block : 2 * block, :] = middle_a_ref[...]
            out_ref[2 * block :, :] = middle_b_ref[...]

    arrays = (near, middle_a, ends_a, middle_b, ends_b)
    return local_call(kernel, like(middle_b, 3 * block, cols), [tensor], *arrays)


def product_rows(features, whole, last, first):
    width = features.shape[0]
    cols = last[0].shape[1]

    def kernel(*refs):
        features_ref, out_ref = refs[-2:]
        for at in range(0, cols, 256):
            here = slice(at, at + 256)
            at_row, total = 0, None
            for ref in refs[:-2]:
                part = jnp.dot(
                    features_ref[:, at_row : at_row + ref.shape[0]], ref[:, here], preferred_element_type=jnp.float32
                )
                total = part if total is None else total + part
                at_row += ref.shape[0]
            out_ref[:, here] = total.astype(out_ref.dtype)

    out = jax.ShapeDtypeStruct((width, cols), jnp.bfloat16)
    column = {i: first // cols for i in range(len(whole))}
    arrays = (*whole, *last, features)
    return local_call(kernel, out, [], *arrays, fetched=True, stored=True, column=column, resident=FAR + 1)


def value_kernel(tensor_ref, query_ref, key_ref, segment_ref, weight_ref, *refs):
    count = FAR * len(CHUNKS)
    whole_refs, last_refs = refs[: -3 - count], refs[-3 - count : -3]
    out_ref, grad_ref, total_ref = refs[-3:]
    length, width = out_ref.shape
    heads = width // HEAD_DIM
    step = min(256, length)
    block = whole_refs[0].shape[0]
    order = block_order(tensor_ref[0])

    def through(blocks, first):
        lhs = jnp.concatenate([ref[...] for ref in blocks], axis=0)
        cols = slice(first, first + lhs.shape[1])
        return lax.dot_general(lhs, weight_ref[:, cols], (((1,), (1,)), ((), ())), preferred_element_type=jnp.float32)

    def put(places, total):
        for i, place in enumerate(places):
            rows = pl.ds(pl.multiple_of(order[place] * block, block), block)
            grad_ref[rows, :] = total[i * block : (i + 1) * block].astype(grad_ref.dtype)

    put(range(2), through(whole_refs, 0))
    total = None
    for i, first in enumerate(FIRSTS):
        piece = through(last_refs[FAR * i : FAR * i + FAR], first)
        total = piece if total is None else total + piece
    put(range(2, 8), total)

    segments = segment_ref[...]
    begin = jnp.zeros_like(segments)
    for id in (0, 1):
        begin = begin + jnp.where(segments > id, jnp.sum((segments == id).astype(jnp.int32), axis=1, keepdims=True), 0)
    scale = HEAD_DIM**-0.5
    for first in range(0, length, step):
        stop = first + step
        key_at = lax.broadcasted_iota(jnp.int32, (stop, step), 0)
        query_at = lax.broadcasted_iota(jnp.int32, (stop, step), 1) + first
        allowed = (key_at <= query_at) & (key_at >= begin[:, first:stop])
        bias = jnp.where(allowed, 0.0, -1e30)
        for head in range(heads):
            cols = slice(head * HEAD_DIM, (head + 1) * HEAD_DIM)
            scores = lax.dot_general(
                key_ref[0:stop, cols],
                query_ref[first:stop, cols],
                (((1,), (1,)), ((), ())),
                preferred_element_type=jnp.float32,
            )
            masked = scores + bias
            highest = jnp.max(masked, axis=0, keepdims=True)
            weights = jnp.exp((masked - highest) * scale)
            inverse = 1.0 / jnp.sum(weights, axis=0, keepdims=True)
            probs = (weights * inverse).astype(grad_ref.dtype)
            update = jnp.dot(probs, grad_ref[first:stop, cols], preferred_element_type=jnp.float32)
            if first > 0:
                total_ref[0:first, cols] = total_ref[0:first, cols] + update[0:first]
            total_ref[first:stop, cols] = update[first:stop]
    out_ref[...] = total_ref[...].astype(out_ref.dtype)


def value_rows(tensor, queries, keys, segments, weight, whole, last):
    length, width = queries.shape
    return local_call(
        value_kernel,
        like(queries, length, width),
        [tensor],
        queries,
        keys,
        segments[None, :],
        weight,
        *whole,
        *last,
        fetched=True,
        stored=True,
        limit=40 << 20,
        scratch=[pltpu.VMEM((length, width), jnp.bfloat16), pltpu.VMEM((length, width), jnp.float32)],
    )


def sum_kernel(*refs):
    out_ref = refs[-1]
    for first, ref in zip(FIRSTS, refs):
        here = slice(first, first + ref.shape[2])
        total = ref[0].astype(jnp.float32)
        for i in range(1, ref.shape[0]):
            total = total + ref[i].astype(jnp.float32)
        out_ref[:, here] = total.astype(out_ref.dtype)


def sum_slabs(chunks):
    out = like(chunks[0], chunks[0].shape[1], sum(CHUNKS))
    return local_call(sum_kernel, out, [], *chunks)


def send(array, pairs):
    return lax.ppermute(array, "tensor", pairs)


def shards(d_out, attn_out, queries, keys, out_weight, segment_ids):
    return step(d_out[0], attn_out[0], queries[0], keys[0], out_weight, segment_ids[0])


def step(whole, outputs, queries, keys, weight, segments):
    index = lax.axis_index("tensor")
    tensor = index.astype(jnp.int32)[None]
    width = outputs.shape[1]
    rows = width // DP
    count = len(CHUNKS)
    own_parts = split(whole)
    near = [send(own_parts[i], PAIRS) for i in range(count)]
    middle_a = [send(own_parts[i], MIDDLE) for i in range(count)]
    features = ordered_features(tensor, outputs)
    full = [whole, send(whole, PARTNER)]
    middle_b = [send(near[i], MIDDLE) for i in range(count)]
    ends_a = [send(middle_a[i], ENDS) for i in range(count)]
    ends_b = [send(middle_b[i], ENDS) for i in range(count)]
    last, moved = [], []
    for i in range(count):
        got = pick(tensor, near[i], middle_a[i], ends_a[i], middle_b[i], ends_b[i])
        pair = [got, send(got, PARTNER)]
        last += pair
        product = product_rows(features, full, pair, FIRSTS[i])
        product = product.reshape(NX, width // NX, CHUNKS[i])
        moved.append(lax.all_to_all(product, "dp", 0, 0, axis_index_groups=GROUPS_X))
    total = sum_slabs(moved).reshape(NY * NZ, rows, whole.shape[1])
    total = lax.all_to_all(total, "dp", 0, 0, axis_index_groups=GROUPS_YZ)
    owned = jnp.sum(total.astype(jnp.float32) * (1 / DP), axis=0)
    values = value_rows(tensor, queries, keys, segments, weight, full, last)
    return values[None], owned


def solution(mesh):
    placed = (
        P("dp", "tensor", None),
        P("dp", None, "tensor"),
        P("dp", None, "tensor"),
        P("dp", None, "tensor"),
        P("tensor", None),
        P("dp", None),
    )
    return jax.shard_map(
        shards,
        mesh=mesh,
        in_specs=placed,
        out_specs=(P("dp", None, "tensor"), P(("tensor", "dp"), None)),
        check_vma=False,
    )
```
